32 devices in a mesh: grp: 4 (over y, core), mem: 8 (over z, x).
Axes of the slice: x: 2, y: 2, z: 4, core: 2. Of those that a mesh axis runs over, the one named last changes fastest.
Arguments:
- video: bfloat16 [32, 32, 32, 1024], P('mem', 'grp'), may hold values from -6 to 6
- w_triple: bfloat16 [2, 1024, 3072], replicated, may hold values from -0.75 to 0.75, as said below
- w_out: bfloat16 [2, 1024, 1024], replicated, may hold values from -0.1875 to 0.1875
Outputs:
- result: bfloat16 [32, 32, 32, 1024], P('mem', 'grp')
The draws below stay inside these ranges and needn't reach their ends.
Inputs may be any that keep to these rules, and one draw needn't show every extreme that they name: `w_triple`: entries of order 1024 ** -0.5, independent between columns of values.
All inputs are finite; a program needn't handle non-finite values.
Results may differ from the reference program's by a relative error of at most 0.008.
Values may be sent and summed in bfloat16 or wider, within the bound.
A program may use at most 128 MiB of HBM per device.

```python
import jax
import jax.numpy as jnp
from jax import lax

D = 1024
HEADS = 16
HEAD = 64
COLS = 32
BLOCKS = 2
FRAMES = 32
ROWS = 32


def draw_video(key, part):
    base = jax.random.normal(key, (FRAMES, ROWS, COLS, D), jnp.float32)
    return jnp.clip(base, -6.0, 6.0).astype(jnp.bfloat16)


def draw_w_triple(key, part):
    weights = jax.random.truncated_normal(key, -4.0, 4.0, (BLOCKS, D, 3 * D), jnp.float32) * D ** (-0.5)
    return weights.astype(jnp.bfloat16)


def gaussian(stream_key, shape, deviation, limit, dtype=jnp.bfloat16):
    return jnp.clip(deviation * jax.random.normal(stream_key, shape, jnp.float32), -limit, limit).astype(dtype)


def setup_inputs(seed: int = 0) -> dict:
    key_of = jax.random.split(jax.random.key(seed), 4)
    video = draw_video(jax.random.fold_in(key_of[3], 71), 0)
    w_triple = draw_w_triple(jax.random.fold_in(key_of[3], 71), 0)
    w_out = gaussian(key_of[2], (BLOCKS, D, D), D ** -0.5, 0.1875)
    return {"video": video, "w_triple": w_triple, "w_out": w_out}


eps = 1e-06
time_forms = ('sabhe,tabhe->abhst', 'abhst,tabhe->sabhe')
height_forms = ('asbhe,atbhe->abhst', 'abhst,atbhe->asbhe')

def attend_full(triple, forms):
    lead = triple.shape[:-1]
    pieces = triple.reshape(lead + (3, HEADS, HEAD)).astype(jnp.float32)
    query = pieces[..., 0, :, :]
    keys = pieces[..., 1, :, :]
    values = pieces[..., 2, :, :]
    scores = jnp.einsum(forms[0], query, keys) * (1.0 / HEAD ** 0.5)
    top = lax.optimization_barrier(jnp.max(scores, axis=-1, keepdims=True))
    expo = jnp.exp(scores - top)
    probs = (expo / lax.optimization_barrier(jnp.sum(expo, axis=-1, keepdims=True))).astype(jnp.bfloat16)
    context = jnp.einsum(forms[1], probs.astype(jnp.float32), values)
    return context.astype(jnp.bfloat16).reshape(lead + (D,))

def reference(video, w_triple, w_out):
    state = video
    for layer in range(BLOCKS):
        forms = time_forms if layer % 2 == 0 else height_forms
        floats = state.astype(jnp.float32)
        normed = (floats * lax.rsqrt(lax.optimization_barrier(jnp.mean(floats * floats, axis=-1, keepdims=True)) + eps)).astype(jnp.bfloat16)
        triple = jnp.dot(normed.reshape(-1, D), w_triple[layer], preferred_element_type=jnp.float32)
        triple = triple.astype(jnp.bfloat16).reshape(state.shape[:-1] + (3 * D,))
        context = attend_full(triple, forms)
        update = jnp.dot(context.reshape(-1, D), w_out[layer], preferred_element_type=jnp.float32)
        state = (floats + update.reshape(floats.shape)).astype(jnp.bfloat16)
    return state
```

```python
import functools

import jax
import jax.numpy as jnp
from jax import lax
from jax.experimental import pallas as pl
from jax.experimental.pallas import tpu as pltpu
from jax.sharding import PartitionSpec as P

HEADS = 16
HEAD = 64
CORES = 2
LANES = 128

eps = 1e-06
MASKED = -1e30
time_forms = ("sabhe,tabhe->abhst", "abhst,tabhe->sabhe")
height_forms = ("asbhe,atbhe->abhst", "abhst,atbhe->asbhe")


def attend_group(state, block, w_in, w_back, bias, normed, context):
    tokens, width = state.shape
    band = min(256, width)
    per_band = band // HEAD
    floats = state.astype(jnp.float32)
    power = jnp.mean(floats * floats, axis=-1, keepdims=True)
    normed[...] = (floats * lax.rsqrt(power + eps)).astype(jnp.bfloat16)
    lane_head = lax.broadcasted_iota(jnp.int32, (tokens, band), 1) // HEAD
    for start in range(0, width, band):
        pieces = [
            jnp.dot(
                normed[...],
                w_in[block, :, which * width + start : which * width + start + band],
                preferred_element_type=jnp.float32,
            ).astype(jnp.bfloat16)
            for which in range(3)
        ]
        query, keys, values = pieces
        alone = jnp.concatenate(
            [jnp.where(lane_head == head, query, jnp.zeros_like(query)) for head in range(per_band)], axis=0
        )
        scores = lax.dot_general(
            alone, keys, (((1,), (1,)), ((), ())), preferred_element_type=jnp.float32
        )
        expos, shares = [], []
        for head in range(per_band):
            block_scores = scores[head * tokens : (head + 1) * tokens] + bias[...]
            top = jnp.max(block_scores, axis=-1, keepdims=True)
            expo = jnp.exp((block_scores - top) * (1.0 / HEAD**0.5))
            shares.append(1.0 / jnp.sum(expo, axis=-1, keepdims=True))
            expos.append(expo.astype(jnp.bfloat16))
        parts = jnp.dot(jnp.concatenate(expos, axis=0), values, preferred_element_type=jnp.float32)
        mixed = parts[:tokens] * shares[0]
        for head in range(1, per_band):
            part = parts[head * tokens : (head + 1) * tokens] * shares[head]
            mixed = jnp.where(lane_head == head, part, mixed)
        context[:, start : start + band] = mixed.astype(jnp.bfloat16)
    update = jnp.dot(context[...], w_back[block], preferred_element_type=jnp.float32)
    return (state.astype(jnp.float32) + update).astype(jnp.bfloat16)


def line_bias(bias, line_of):
    shape = bias.shape
    first = line_of(lax.broadcasted_iota(jnp.int32, shape, 0))
    second = line_of(lax.broadcasted_iota(jnp.int32, shape, 1))
    bias[...] = jnp.where(first == second, 0.0, MASKED).astype(jnp.float32)


def split_lanes(rows):
    return jnp.stack([rows[:, at : at + LANES] for at in range(0, rows.shape[1], LANES)])


LEVELS = 4
SAME, HALF, LOWER, UPPER = 0, 1, 2, 3
INNER_ORDER = (
    (LOWER, 0, 0), (UPPER, 0, 0), (LOWER, 0, 1), (UPPER, 0, 1), (HALF, 0, 0), (SAME, 0, 0), (HALF, 0, 1), (SAME, 0, 1),
    (LOWER, 1, 0), (UPPER, 1, 0), (LOWER, 1, 1), (UPPER, 1, 1), (HALF, 1, 0), (SAME, 1, 0), (HALF, 1, 1), (SAME, 1, 1),
)
OUTER_ORDER = (
    (HALF, 0, 0), (HALF, 0, 1), (HALF, 1, 0), (HALF, 1, 1), (LOWER, 0, 0), (UPPER, 0, 0), (SAME, 0, 0), (LOWER, 0, 1),
    (UPPER, 0, 1), (SAME, 0, 1), (SAME, 1, 0), (SAME, 1, 1), (LOWER, 1, 0), (UPPER, 1, 0), (LOWER, 1, 1), (UPPER, 1, 1),
)
HELD = 4
HELD_TURNS = 2


def looked_up(at, table):
    found = table[0]
    for index in range(1, len(table)):
        found = jnp.where(at == index, table[index], found)
    return found


def level_of(kind, level):
    near = level + kind - 2 * kind * (level % 2)
    far = (1 - level // 2) * 2 + kind - LOWER
    return jnp.where(kind < LOWER, near, far)


def column_kernel(
    mems, grps, frames, rows, steps,
    x_ref, w_in_hbm, w_back_hbm, out_ref,
    tokens_in, wide, apart, held, w_in, w_back, bias, normed, context,
    x_sem, w_sem, send_in, recv_in, send_out, recv_out, go,
):
    places = mems * grps
    small, width = held.shape[1], held.shape[2]
    per_step = mems // steps
    my_mem, my_grp = lax.axis_index("mem"), lax.axis_index("grp")
    me = my_mem * grps + my_grp
    my_pair, my_part = my_grp // CORES, my_mem // per_step
    outer = (my_part + my_part // 2) % 2 == 0

    arrive = pltpu.make_async_copy(x_ref, tokens_in, x_sem)
    arrive.start()
    weights = []
    for block in range(2):
        weights.append(pltpu.make_async_copy(w_in_hbm.at[block], w_in.at[block], w_sem.at[block, 0]))
        weights.append(pltpu.make_async_copy(w_back_hbm.at[block], w_back.at[block], w_sem.at[block, 1]))
    barrier = pltpu.get_barrier_semaphore()

    @pl.loop(1, places)
    def _(offset):
        other = (me + offset) % places
        pl.semaphore_signal(barrier, inc=1, device_id={"mem": other // grps, "grp": other % grps})

    arrive.wait()
    for copy in weights:
        copy.start()

    @pl.loop(0, small)
    def _(at):
        wide[:, pl.ds(pl.multiple_of(at * places, places), places), :] = split_lanes(
            tokens_in[at].astype(jnp.float32)
        )

    pl.semaphore_wait(barrier, places - 1)

    def inward(place):
        return pltpu.make_async_remote_copy(
            src_ref=apart.at[place],
            dst_ref=held.at[me],
            send_sem=send_in.at[place],
            recv_sem=recv_in.at[me],
            device_id={"mem": place // grps, "grp": place % grps},
        )

    def place_of(at):
        turn = at // per_step
        kind, core, pair = (
            jnp.where(outer, looked_up(turn, [a[k] for a in OUTER_ORDER]), looked_up(turn, [a[k] for a in INNER_ORDER]))
            for k in range(3)
        )
        to_pair = (my_pair + pair) % (grps // CORES)
        to_mem = level_of(kind, my_part) * per_step + (my_mem + at) % per_step
        return to_mem * grps + to_pair * CORES + core

    held_back = places - places // HELD
    my_core = my_grp % CORES

    def start_held():
        @pl.loop(held_back, places)
        def _(at):
            inward(place_of(at)).start()

    @pl.loop(0, places)
    def _(at):
        place = place_of(at)
        for lane in range(wide.shape[0]):
            column = wide[lane, pl.ds(place, small, stride=places), :]
            apart[place, :, lane * LANES : (lane + 1) * LANES] = column.astype(apart.dtype)

        @pl.when(place == me)
        def _():
            pltpu.make_async_copy(apart.at[me], held.at[me], recv_in.at[me]).start()

        @pl.when((place != me) & ~(outer & (at >= held_back)))
        def _():
            inward(place).start()

    @pl.when(outer & (my_core == 1))
    def _():
        pl.semaphore_wait(go, 1)
        start_held()

    line_bias(bias, lambda at: at % rows)
    weights[0].wait()
    weights[1].wait()

    @pl.loop(0, grps)
    def _(turn):
        pair = (my_pair + turn // CORES) % (grps // CORES)
        grp = pair * CORES + (my_grp + turn) % CORES

        @pl.loop(0, mems)
        def _(mem):
            place = mem * grps + grp
            pltpu.make_async_copy(apart.at[place], held.at[place], recv_in.at[place]).wait()

        state = jnp.concatenate([held[mem * grps + grp] for mem in range(mems)], axis=0)
        done = attend_group(state, 0, w_in, w_back, bias, normed, context)
        for mem in range(mems):
            held[mem * grps + grp] = done[mem * small : (mem + 1) * small]

        @pl.when(outer & (my_core == 0) & (turn == HELD_TURNS - 1))
        def _():
            pl.semaphore_signal(go, inc=1, device_id={"mem": my_mem, "grp": my_grp + 1})
            start_held()

    line_bias(bias, lambda at: at // (grps * small) * frames + at // rows % frames)
    weights[2].wait()
    weights[3].wait()

    def outward(place):
        return pltpu.make_async_remote_copy(
            src_ref=held.at[place],
            dst_ref=out_ref.at[me],
            send_sem=send_out.at[place],
            recv_sem=recv_out.at[me],
            device_id={"mem": place // grps, "grp": place % grps},
        )

    count = per_step * grps

    @pl.loop(0, steps)
    def _(turn):
        late = outer & (my_core == 0)
        kind = jnp.where(
            late, looked_up(turn, [HALF, LOWER, UPPER, SAME]), looked_up(turn, [LOWER, UPPER, HALF, SAME])
        )
        step = level_of(kind, my_part)
        first = step * count
        state = jnp.concatenate([held[first + at] for at in range(count)], axis=0)
        done = attend_group(state, 1, w_in, w_back, bias, normed, context)
        for at in range(count):
            held[first + at] = done[at * small : (at + 1) * small]

        @pl.loop(0, count)
        def _(at):
            to_mem = (my_mem + at // grps) % per_step
            to_pair = (my_pair + at % grps // CORES) % (grps // CORES)
            place = first + to_mem * grps + to_pair * CORES + (my_core + at) % CORES

            @pl.when(place == me)
            def _():
                pltpu.make_async_copy(held.at[me], out_ref.at[me], recv_out.at[me]).start()

            @pl.when(place != me)
            def _():
                outward(place).start()

    @pl.loop(1, places)
    def _(offset):
        place = (me + offset) % places
        inward(place).wait_send()
        outward(place).wait_send()

    @pl.loop(0, places)
    def _(place):
        pltpu.make_async_copy(held.at[place], out_ref.at[place], recv_out.at[place]).wait()


def by_column(mems, grps, video, w_triple, w_out):
    frames, rows, cols, width = video.shape
    places, small = mems * grps, frames * rows
    steps = LEVELS
    tokens = mems * small
    dma = pltpu.SemaphoreType.DMA
    back = pl.pallas_call(
        functools.partial(column_kernel, mems, grps, frames, rows, steps),
        out_shape=jax.ShapeDtypeStruct((places, small, width), video.dtype),
        in_specs=[pl.BlockSpec(memory_space=pl.ANY)] * 3,
        out_specs=pl.BlockSpec(memory_space=pl.ANY),
        scratch_shapes=[
            pltpu.VMEM((small, places, width), video.dtype),
            pltpu.VMEM((width // LANES, small * places, LANES), jnp.float32),
            pltpu.VMEM((places, small, width), video.dtype),
            pltpu.VMEM((places, small, width), video.dtype),
            pltpu.VMEM(w_triple.shape, w_triple.dtype),
            pltpu.VMEM(w_out.shape, w_out.dtype),
            pltpu.VMEM((tokens, tokens), jnp.float32),
            pltpu.VMEM((tokens, width), video.dtype),
            pltpu.VMEM((tokens, width), video.dtype),
            dma,
            dma((2, 2)),
            dma((places,)),
            dma((places,)),
            dma((places,)),
            dma((places,)),
            pltpu.SemaphoreType.REGULAR,
        ],
        compiler_params=pltpu.CompilerParams(
            collective_id=0, has_side_effects=True, vmem_limit_bytes=60 * 2**20
        ),
    )(video.reshape(small, cols, width), w_triple, w_out)
    return jnp.transpose(back.reshape(cols, frames, rows, width), (1, 2, 0, 3))


def attend_local(triple, forms):
    lead = triple.shape[:-1]
    width = triple.shape[-1] // 3
    pieces = triple.reshape(lead + (3, HEADS, HEAD))
    query = pieces[..., 0, :, :]
    keys = pieces[..., 1, :, :]
    values = pieces[..., 2, :, :]
    scores = jnp.einsum(forms[0], query, keys, preferred_element_type=jnp.float32) * (
        1.0 / HEAD**0.5
    )
    top = jnp.max(scores, axis=-1, keepdims=True)
    expo = jnp.exp(scores - top)
    probs = (expo / jnp.sum(expo, axis=-1, keepdims=True)).astype(jnp.bfloat16)
    context = jnp.einsum(forms[1], probs, values, preferred_element_type=jnp.float32)
    return context.astype(jnp.bfloat16).reshape(lead + (width,))


def make_triple(state, weight_in):
    width = state.shape[-1]
    floats = state.astype(jnp.float32)
    normed = (floats * lax.rsqrt(jnp.mean(floats * floats, axis=-1, keepdims=True) + eps)).astype(
        jnp.bfloat16
    )
    triple = jnp.dot(normed.reshape(-1, width), weight_in, preferred_element_type=jnp.float32)
    return triple.astype(jnp.bfloat16).reshape(state.shape[:-1] + (3 * width,))


def add_update(state, context, weight_back):
    width = state.shape[-1]
    update = jnp.dot(context.reshape(-1, width), weight_back, preferred_element_type=jnp.float32)
    return (state.astype(jnp.float32) + update.reshape(state.shape)).astype(jnp.bfloat16)


def whole_block(state, weight_in, weight_back, forms):
    context = attend_local(make_triple(state, weight_in), forms)
    return add_update(state, context, weight_back)


def by_lines(video, w_triple, w_out):
    regrouped = whole_block(
        lax.all_to_all(video, "mem", split_axis=2, concat_axis=0, tiled=True),
        w_triple[0],
        w_out[0],
        time_forms,
    )
    height_done = whole_block(
        lax.all_to_all(regrouped, "grp", split_axis=0, concat_axis=1, tiled=True),
        w_triple[1],
        w_out[1],
        height_forms,
    )
    return lax.all_to_all(
        lax.all_to_all(height_done, "grp", split_axis=1, concat_axis=0, tiled=True),
        "mem",
        split_axis=0,
        concat_axis=2,
        tiled=True,
    )


def solution(mesh):
    mems, grps = mesh.shape["mem"], mesh.shape["grp"]

    def on_device(video, w_triple, w_out):
        if video.shape[2] == mems * grps and mems == 4 * (mems // 4) == (mems // 4) * grps and grps % CORES == 0:
            return by_column(mems, grps, video, w_triple, w_out)
        return by_lines(video, w_triple, w_out)

    return jax.shard_map(
        on_device,
        mesh=mesh,
        in_specs=(P("mem", "grp", None, None), P(), P()),
        out_specs=P("mem", "grp", None, None),
        check_vma=False,
    )
```

```python
import functools

import jax
import jax.numpy as jnp
from jax import lax
from jax.experimental import pallas as pl
from jax.experimental.pallas import tpu as pltpu
from jax.sharding import PartitionSpec as P

HEADS = 16
HEAD = 64
CORES = 2
LANES = 128

eps = 1e-06
MASKED = -1e30
time_forms = ("sabhe,tabhe->abhst", "abhst,tabhe->sabhe")
height_forms = ("asbhe,atbhe->abhst", "abhst,atbhe->asbhe")


def attend_group(state, block, w_in, w_back, bias, normed, context):
    tokens, width = state.shape
    band = min(256, width)
    per_band = band // HEAD
    floats = state.astype(jnp.float32)
    power = jnp.mean(floats * floats, axis=-1, keepdims=True)
    normed[...] = (floats * lax.rsqrt(power + eps)).astype(jnp.bfloat16)
    lane_head = lax.broadcasted_iota(jnp.int32, (tokens, band), 1) // HEAD
    for start in range(0, width, band):
        pieces = [
            jnp.dot(
                normed[...],
                w_in[block, :, which * width + start : which * width + start + band],
                preferred_element_type=jnp.float32,
            ).astype(jnp.bfloat16)
            for which in range(3)
        ]
        query, keys, values = pieces
        alone = jnp.concatenate(
            [jnp.where(lane_head == head, query, jnp.zeros_like(query)) for head in range(per_band)], axis=0
        )
        scores = lax.dot_general(
            alone, keys, (((1,), (1,)), ((), ())), preferred_element_type=jnp.float32
        )
        expos, shares = [], []
        for head in range(per_band):
            block_scores = scores[head * tokens : (head + 1) * tokens] + bias[...]
            top = jnp.max(block_scores, axis=-1, keepdims=True)
            expo = jnp.exp((block_scores - top) * (1.0 / HEAD**0.5))
            shares.append(1.0 / jnp.sum(expo, axis=-1, keepdims=True))
            expos.append(expo.astype(jnp.bfloat16))
        parts = jnp.dot(jnp.concatenate(expos, axis=0), values, preferred_element_type=jnp.float32)
        mixed = parts[:tokens] * shares[0]
        for head in range(1, per_band):
            part = parts[head * tokens : (head + 1) * tokens] * shares[head]
            mixed = jnp.where(lane_head == head, part, mixed)
        context[:, start : start + band] = mixed.astype(jnp.bfloat16)
    update = jnp.dot(context[...], w_back[block], preferred_element_type=jnp.float32)
    return (state.astype(jnp.float32) + update).astype(jnp.bfloat16)


def line_bias(bias, line_of):
    shape = bias.shape
    first = line_of(lax.broadcasted_iota(jnp.int32, shape, 0))
    second = line_of(lax.broadcasted_iota(jnp.int32, shape, 1))
    bias[...] = jnp.where(first == second, 0.0, MASKED).astype(jnp.float32)


def split_lanes(rows):
    return jnp.stack([rows[:, at : at + LANES] for at in range(0, rows.shape[1], LANES)])


LEVELS = 4
SAME, HALF, LOWER, UPPER = 0, 1, 2, 3
INNER_ORDER = (
    (LOWER, 0, 0), (UPPER, 0, 0), (LOWER, 0, 1), (UPPER, 0, 1), (HALF, 0, 0), (SAME, 0, 0), (HALF, 0, 1), (SAME, 0, 1),
    (LOWER, 1, 0), (UPPER, 1, 0), (LOWER, 1, 1), (UPPER, 1, 1), (HALF, 1, 0), (SAME, 1, 0), (HALF, 1, 1), (SAME, 1, 1),
)
OUTER_ORDER = (
    (HALF, 0, 0), (HALF, 0, 1), (HALF, 1, 0), (HALF, 1, 1), (LOWER, 0, 0), (UPPER, 0, 0), (SAME, 0, 0), (LOWER, 0, 1),
    (UPPER, 0, 1), (SAME, 0, 1), (SAME, 1, 0), (SAME, 1, 1), (LOWER, 1, 0), (UPPER, 1, 0), (LOWER, 1, 1), (UPPER, 1, 1),
)
HELD = 4
HELD_TURNS = 2


def looked_up(at, table):
    found = table[0]
    for index in range(1, len(table)):
        found = jnp.where(at == index, table[index], found)
    return found


def level_of(kind, level):
    near = level + kind - 2 * kind * (level % 2)
    far = (1 - level // 2) * 2 + kind - LOWER
    return jnp.where(kind < LOWER, near, far)


def column_kernel(
    mems, grps, frames, rows, steps,
    x_ref, w_in_hbm, w_back_hbm, out_ref,
    tokens_in, wide, apart, held, w_in, w_back, bias, normed, context,
    x_sem, w_sem, send_in, recv_in, send_out, recv_out, go,
):
    places = mems * grps
    small, width = held.shape[1], held.shape[2]
    per_step = mems // steps
    my_mem, my_grp = lax.axis_index("mem"), lax.axis_index("grp")
    me = my_mem * grps + my_grp
    my_pair, my_part = my_grp // CORES, my_mem // per_step
    outer = (my_part + my_part // 2) % 2 == 0

    arrive = pltpu.make_async_copy(x_ref, tokens_in, x_sem)
    arrive.start()
    weights = []
    for block in range(2):
        weights.append(pltpu.make_async_copy(w_in_hbm.at[block], w_in.at[block], w_sem.at[block, 0]))
        weights.append(pltpu.make_async_copy(w_back_hbm.at[block], w_back.at[block], w_sem.at[block, 1]))
    barrier = pltpu.get_barrier_semaphore()

    @pl.loop(1, places)
    def _(offset):
        other = (me + offset) % places
        pl.semaphore_signal(barrier, inc=1, device_id={"mem": other // grps, "grp": other % grps})

    arrive.wait()
    for copy in weights:
        copy.start()

    @pl.loop(0, small)
    def _(at):
        wide[:, pl.ds(pl.multiple_of(at * places, places), places), :] = split_lanes(
            tokens_in[at].astype(jnp.float32)
        )

    pl.semaphore_wait(barrier, places - 1)

    def inward(place):
        return pltpu.make_async_remote_copy(
            src_ref=apart.at[place],
            dst_ref=held.at[me],
            send_sem=send_in.at[place],
            recv_sem=recv_in.at[me],
            device_id={"mem": place // grps, "grp": place % grps},
        )

    def place_of(at):
        turn = at // per_step
        kind, core, pair = (
            jnp.where(outer, looked_up(turn, [a[k] for a in OUTER_ORDER]), looked_up(turn, [a[k] for a in INNER_ORDER]))
            for k in range(3)
        )
        to_pair = (my_pair + pair) % (grps // CORES)
        to_mem = level_of(kind, my_part) * per_step + (my_mem + at) % per_step
        return to_mem * grps + to_pair * CORES + core

    held_back = places - places // HELD
    my_core = my_grp % CORES

    def start_held():
        @pl.loop(held_back, places)
        def _(at):
            inward(place_of(at)).start()

    @pl.loop(0, places)
    def _(at):
        place = place_of(at)
        for lane in range(wide.shape[0]):
            column = wide[lane, pl.ds(place, small, stride=places), :]
            apart[place, :, lane * LANES : (lane + 1) * LANES] = column.astype(apart.dtype)

        @pl.when(place == me)
        def _():
            pltpu.make_async_copy(apart.at[me], held.at[me], recv_in.at[me]).start()

        @pl.when((place != me) & ~(outer & (at >= held_back)))
        def _():
            inward(place).start()

    @pl.when(outer & (my_core == 1))
    def _():
        pl.semaphore_wait(go, 1)
        start_held()

    line_bias(bias, lambda at: at % rows)
    weights[0].wait()
    weights[1].wait()

    @pl.loop(0, grps)
    def _(turn):
        pair = (my_pair + turn // CORES) % (grps // CORES)
        grp = pair * CORES + (my_grp + turn) % CORES

        @pl.loop(0, mems)
        def _(mem):
            place = mem * grps + grp
            pltpu.make_async_copy(apart.at[place], held.at[place], recv_in.at[place]).wait()

        state = jnp.concatenate([held[mem * grps + grp] for mem in range(mems)], axis=0)
        done = attend_group(state, 0, w_in, w_back, bias, normed, context)
        for mem in range(mems):
            held[mem * grps + grp] = done[mem * small : (mem + 1) * small]

        @pl.when(outer & (my_core == 0) & (turn == HELD_TURNS - 1))
        def _():
            pl.semaphore_signal(go, inc=1, device_id={"mem": my_mem, "grp": my_grp + 1})
            start_held()

    line_bias(bias, lambda at: at // (grps * small) * frames + at // rows % frames)
    weights[2].wait()
    weights[3].wait()

    def outward(place):
        return pltpu.make_async_remote_copy(
            src_ref=held.at[place],
            dst_ref=out_ref.at[me],
            send_sem=send_out.at[place],
            recv_sem=recv_out.at[me],
            device_id={"mem": place // grps, "grp": place % grps},
        )

    count = per_step * grps

    @pl.loop(0, steps)
    def _(turn):
        late = outer & (my_core == 0)
        kind = jnp.where(
            late, looked_up(turn, [HALF, LOWER, UPPER, SAME]), looked_up(turn, [LOWER, UPPER, HALF, SAME])
        )
        step = level_of(kind, my_part)
        first = step * count
        state = jnp.concatenate([held[first + at] for at in range(count)], axis=0)
        done = attend_group(state, 1, w_in, w_back, bias, normed, context)
        for at in range(count):
            held[first + at] = done[at * small : (at + 1) * small]

        @pl.loop(0, count)
        def _(at):
            to_mem = (my_mem + at // grps) % per_step
            to_pair = (my_pair + at % grps // CORES) % (grps // CORES)
            place = first + to_mem * grps + to_pair * CORES + (my_core + at) % CORES

            @pl.when(place == me)
            def _():
                pltpu.make_async_copy(held.at[me], out_ref.at[me], recv_out.at[me]).start()

            @pl.when(place != me)
            def _():
                outward(place).start()

    @pl.loop(1, places)
    def _(offset):
        place = (me + offset) % places
        inward(place).wait_send()
        outward(place).wait_send()

    @pl.loop(0, places)
    def _(place):
        pltpu.make_async_copy(held.at[place], out_ref.at[place], recv_out.at[place]).wait()


def by_column(mems, grps, video, w_triple, w_out):
    frames, rows, cols, width = video.shape
    places, small = mems * grps, frames * rows
    steps = LEVELS
    tokens = mems * small
    dma = pltpu.SemaphoreType.DMA
    back = pl.pallas_call(
        functools.partial(column_kernel, mems, grps, frames, rows, steps),
        out_shape=jax.ShapeDtypeStruct((places, small, width), video.dtype),
        in_specs=[pl.BlockSpec(memory_space=pl.ANY)] * 3,
        out_specs=pl.BlockSpec(memory_space=pl.ANY),
        scratch_shapes=[
            pltpu.VMEM((small, places, width), video.dtype),
            pltpu.VMEM((width // LANES, small * places, LANES), jnp.float32),
            pltpu.VMEM((places, small, width), video.dtype),
            pltpu.VMEM((places, small, width), video.dtype),
            pltpu.VMEM(w_triple.shape, w_triple.dtype),
            pltpu.VMEM(w_out.shape, w_out.dtype),
            pltpu.VMEM((tokens, tokens), jnp.float32),
            pltpu.VMEM((tokens, width), video.dtype),
            pltpu.VMEM((tokens, width), video.dtype),
            dma,
            dma((2, 2)),
            dma((places,)),
            dma((places,)),
            dma((places,)),
            dma((places,)),
            pltpu.SemaphoreType.REGULAR,
        ],
        compiler_params=pltpu.CompilerParams(
            collective_id=0, has_side_effects=True, vmem_limit_bytes=50 * 2**20
        ),
    )(video.reshape(small, cols, width), w_triple, w_out)
    return jnp.transpose(back.reshape(cols, frames, rows, width), (1, 2, 0, 3))


def attend_local(triple, forms):
    lead = triple.shape[:-1]
    width = triple.shape[-1] // 3
    pieces = triple.reshape(lead + (3, HEADS, HEAD))
    query = pieces[..., 0, :, :]
    keys = pieces[..., 1, :, :]
    values = pieces[..., 2, :, :]
    scores = jnp.einsum(forms[0], query, keys, preferred_element_type=jnp.float32) * (
        1.0 / HEAD**0.5
    )
    top = jnp.max(scores, axis=-1, keepdims=True)
    expo = jnp.exp(scores - top)
    probs = (expo / jnp.sum(expo, axis=-1, keepdims=True)).astype(jnp.bfloat16)
    context = jnp.einsum(forms[1], probs, values, preferred_element_type=jnp.float32)
    return context.astype(jnp.bfloat16).reshape(lead + (width,))


def make_triple(state, weight_in):
    width = state.shape[-1]
    floats = state.astype(jnp.float32)
    normed = (floats * lax.rsqrt(jnp.mean(floats * floats, axis=-1, keepdims=True) + eps)).astype(
        jnp.bfloat16
    )
    triple = jnp.dot(normed.reshape(-1, width), weight_in, preferred_element_type=jnp.float32)
    return triple.astype(jnp.bfloat16).reshape(state.shape[:-1] + (3 * width,))


def add_update(state, context, weight_back):
    width = state.shape[-1]
    update = jnp.dot(context.reshape(-1, width), weight_back, preferred_element_type=jnp.float32)
    return (state.astype(jnp.float32) + update.reshape(state.shape)).astype(jnp.bfloat16)


def whole_block(state, weight_in, weight_back, forms):
    context = attend_local(make_triple(state, weight_in), forms)
    return add_update(state, context, weight_back)


def by_lines(video, w_triple, w_out):
    regrouped = whole_block(
        lax.all_to_all(video, "mem", split_axis=2, concat_axis=0, tiled=True),
        w_triple[0],
        w_out[0],
        time_forms,
    )
    height_done = whole_block(
        lax.all_to_all(regrouped, "grp", split_axis=0, concat_axis=1, tiled=True),
        w_triple[1],
        w_out[1],
        height_forms,
    )
    return lax.all_to_all(
        lax.all_to_all(height_done, "grp", split_axis=1, concat_axis=0, tiled=True),
        "mem",
        split_axis=0,
        concat_axis=2,
        tiled=True,
    )


def solution(mesh):
    mems, grps = mesh.shape["mem"], mesh.shape["grp"]

    def on_device(video, w_triple, w_out):
        if video.shape[2] == mems * grps and mems == 4 * (mems // 4) == (mems // 4) * grps and grps % CORES == 0:
            return by_column(mems, grps, video, w_triple, w_out)
        return by_lines(video, w_triple, w_out)

    return jax.shard_map(
        on_device,
        mesh=mesh,
        in_specs=(P("mem", "grp", None, None), P(), P()),
        out_specs=P("mem", "grp", None, None),
        check_vma=False,
    )
```

```python
import functools

import jax
import jax.numpy as jnp
from jax import lax
from jax.experimental import pallas as pl
from jax.experimental.pallas import tpu as pltpu
from jax.sharding import PartitionSpec as P

HEADS = 16
HEAD = 64
CORES = 2
LANES = 128

eps = 1e-06
MASKED = -1e30
time_forms = ("sabhe,tabhe->abhst", "abhst,tabhe->sabhe")
height_forms = ("asbhe,atbhe->abhst", "abhst,atbhe->asbhe")


def attend_group(state, block, w_in, w_back, bias, normed, context):
    tokens, width = state.shape
    band = min(256, width)
    per_band = band // HEAD
    floats = state.astype(jnp.float32)
    power = jnp.mean(floats * floats, axis=-1, keepdims=True)
    normed[...] = (floats * lax.rsqrt(power + eps)).astype(jnp.bfloat16)
    lane_head = lax.broadcasted_iota(jnp.int32, (tokens, band), 1) // HEAD
    for start in range(0, width, band):
        pieces = [
            jnp.dot(
                normed[...],
                w_in[block, :, which * width + start : which * width + start + band],
                preferred_element_type=jnp.float32,
            ).astype(jnp.bfloat16)
            for which in range(3)
        ]
        query, keys, values = pieces
        alone = jnp.concatenate(
            [jnp.where(lane_head == head, query, jnp.zeros_like(query)) for head in range(per_band)], axis=0
        )
        scores = lax.dot_general(
            alone, keys, (((1,), (1,)), ((), ())), preferred_element_type=jnp.float32
        )
        expos, shares = [], []
        for head in range(per_band):
            block_scores = scores[head * tokens : (head + 1) * tokens] + bias[...]
            top = jnp.max(block_scores, axis=-1, keepdims=True)
            expo = jnp.exp((block_scores - top) * (1.0 / HEAD**0.5))
            shares.append(1.0 / jnp.sum(expo, axis=-1, keepdims=True))
            expos.append(expo.astype(jnp.bfloat16))
        parts = jnp.dot(jnp.concatenate(expos, axis=0), values, preferred_element_type=jnp.float32)
        mixed = parts[:tokens] * shares[0]
        for head in range(1, per_band):
            part = parts[head * tokens : (head + 1) * tokens] * shares[head]
            mixed = jnp.where(lane_head == head, part, mixed)
        context[:, start : start + band] = mixed.astype(jnp.bfloat16)
    update = jnp.dot(context[...], w_back[block], preferred_element_type=jnp.float32)
    return (state.astype(jnp.float32) + update).astype(jnp.bfloat16)


def line_bias(bias, line_of):
    shape = bias.shape
    first = line_of(lax.broadcasted_iota(jnp.int32, shape, 0))
    second = line_of(lax.broadcasted_iota(jnp.int32, shape, 1))
    bias[...] = jnp.where(first == second, 0.0, MASKED).astype(jnp.float32)


def split_lanes(rows):
    return jnp.stack([rows[:, at : at + LANES] for at in range(0, rows.shape[1], LANES)])


LEVELS = 4
SAME, HALF, LOWER, UPPER = 0, 1, 2, 3
INNER_ORDER = (
    (LOWER, 0, 0), (UPPER, 0, 0), (LOWER, 0, 1), (UPPER, 0, 1), (HALF, 0, 0), (SAME, 0, 0), (HALF, 0, 1), (SAME, 0, 1),
    (LOWER, 1, 0), (UPPER, 1, 0), (LOWER, 1, 1), (UPPER, 1, 1), (HALF, 1, 0), (SAME, 1, 0), (HALF, 1, 1), (SAME, 1, 1),
)
OUTER_ORDER = (
    (HALF, 0, 0), (HALF, 0, 1), (HALF, 1, 0), (HALF, 1, 1), (LOWER, 0, 0), (UPPER, 0, 0), (SAME, 0, 0), (LOWER, 0, 1),
    (UPPER, 0, 1), (SAME, 0, 1), (SAME, 1, 0), (SAME, 1, 1), (LOWER, 1, 0), (UPPER, 1, 0), (LOWER, 1, 1), (UPPER, 1, 1),
)
HELD = 4
HELD_TURNS = 2


def looked_up(at, table):
    found = table[0]
    for index in range(1, len(table)):
        found = jnp.where(at == index, table[index], found)
    return found


def level_of(kind, level):
    near = level + kind - 2 * kind * (level % 2)
    far = (1 - level // 2) * 2 + kind - LOWER
    return jnp.where(kind < LOWER, near, far)


def column_kernel(
    mems, grps, frames, rows, steps,
    x_ref, w_in_hbm, w_back_hbm, out_ref,
    tokens_in, wide, apart, held, w_in, w_back, bias, normed, context,
    x_sem, w_sem, send_in, recv_in, send_out, recv_out, go,
):
    places = mems * grps
    small, width = held.shape[1], held.shape[2]
    per_step = mems // steps
    my_mem, my_grp = lax.axis_index("mem"), lax.axis_index("grp")
    me = my_mem * grps + my_grp
    my_pair, my_part = my_grp // CORES, my_mem // per_step
    outer = (my_part + my_part // 2) % 2 == 0

    arrive = pltpu.make_async_copy(x_ref, tokens_in, x_sem)
    arrive.start()
    weights = []
    for block in range(2):
        weights.append(pltpu.make_async_copy(w_in_hbm.at[block], w_in.at[block], w_sem.at[block, 0]))
        weights.append(pltpu.make_async_copy(w_back_hbm.at[block], w_back.at[block], w_sem.at[block, 1]))
    barrier = pltpu.get_barrier_semaphore()

    @pl.loop(1, places)
    def _(offset):
        other = (me + offset) % places
        pl.semaphore_signal(barrier, inc=1, device_id={"mem": other // grps, "grp": other % grps})

    arrive.wait()
    for copy in weights:
        copy.start()

    @pl.loop(0, small)
    def _(at):
        wide[:, pl.ds(pl.multiple_of(at * places, places), places), :] = split_lanes(
            tokens_in[at].astype(jnp.float32)
        )

    pl.semaphore_wait(barrier, places - 1)

    def inward(place):
        return pltpu.make_async_remote_copy(
            src_ref=apart.at[place],
            dst_ref=held.at[me],
            send_sem=send_in.at[place],
            recv_sem=recv_in.at[me],
            device_id={"mem": place // grps, "grp": place % grps},
        )

    def place_of(at):
        turn = at // per_step
        kind, core, pair = (
            jnp.where(outer, looked_up(turn, [a[k] for a in OUTER_ORDER]), looked_up(turn, [a[k] for a in INNER_ORDER]))
            for k in range(3)
        )
        to_pair = (my_pair + pair) % (grps // CORES)
        to_mem = level_of(kind, my_part) * per_step + (my_mem + at) % per_step
        return to_mem * grps + to_pair * CORES + core

    held_back = places - places // HELD
    my_core = my_grp % CORES

    def start_held():
        @pl.loop(held_back, places)
        def _(at):
            inward(place_of(at)).start()

    @pl.loop(0, places)
    def _(at):
        place = place_of(at)
        for lane in range(wide.shape[0]):
            column = wide[lane, pl.ds(place, small, stride=places), :]
            apart[place, :, lane * LANES : (lane + 1) * LANES] = column.astype(apart.dtype)

        @pl.when(place == me)
        def _():
            pltpu.make_async_copy(apart.at[me], held.at[me], recv_in.at[me]).start()

        @pl.when((place != me) & ~(outer & (at >= held_back)))
        def _():
            inward(place).start()

    @pl.when(outer & (my_core == 1))
    def _():
        pl.semaphore_wait(go, 1)
        start_held()

    line_bias(bias, lambda at: at % rows)
    weights[0].wait()
    weights[1].wait()

    @pl.loop(0, grps)
    def _(turn):
        pair = (my_pair + turn // CORES) % (grps // CORES)
        grp = pair * CORES + (my_grp + turn) % CORES

        @pl.loop(0, mems)
        def _(mem):
            place = mem * grps + grp
            pltpu.make_async_copy(apart.at[place], held.at[place], recv_in.at[place]).wait()

        state = jnp.concatenate([held[mem * grps + grp] for mem in range(mems)], axis=0)
        done = attend_group(state, 0, w_in, w_back, bias, normed, context)
        for mem in range(mems):
            held[mem * grps + grp] = done[mem * small : (mem + 1) * small]

        @pl.when(outer & (my_core == 0) & (turn == HELD_TURNS - 1))
        def _():
            pl.semaphore_signal(go, inc=1, device_id={"mem": my_mem, "grp": my_grp + 1})
            start_held()

    line_bias(bias, lambda at: at // (grps * small) * frames + at // rows % frames)
    weights[2].wait()
    weights[3].wait()

    def outward(place):
        return pltpu.make_async_remote_copy(
            src_ref=held.at[place],
            dst_ref=out_ref.at[me],
            send_sem=send_out.at[place],
            recv_sem=recv_out.at[me],
            device_id={"mem": place // grps, "grp": place % grps},
        )

    count = per_step * grps

    @pl.loop(0, steps)
    def _(turn):
        late = outer & (my_core == 0)
        kind = jnp.where(
            late, looked_up(turn, [HALF, LOWER, UPPER, SAME]), looked_up(turn, [LOWER, UPPER, HALF, SAME])
        )
        step = level_of(kind, my_part)
        first = step * count
        state = jnp.concatenate([held[first + at] for at in range(count)], axis=0)
        done = attend_group(state, 1, w_in, w_back, bias, normed, context)
        for at in range(count):
            held[first + at] = done[at * small : (at + 1) * small]

        @pl.loop(0, count)
        def _(at):
            to_mem = (my_mem + at) % per_step
            to_pair = (my_pair + at // per_step) % (grps // CORES)
            place = first + to_mem * grps + to_pair * CORES + (my_core + at // grps) % CORES

            @pl.when(place == me)
            def _():
                pltpu.make_async_copy(held.at[me], out_ref.at[me], recv_out.at[me]).start()

            @pl.when(place != me)
            def _():
                outward(place).start()

    @pl.loop(1, places)
    def _(offset):
        place = (me + offset) % places
        inward(place).wait_send()
        outward(place).wait_send()

    @pl.loop(0, places)
    def _(place):
        pltpu.make_async_copy(held.at[place], out_ref.at[place], recv_out.at[place]).wait()


def by_column(mems, grps, video, w_triple, w_out):
    frames, rows, cols, width = video.shape
    places, small = mems * grps, frames * rows
    steps = LEVELS
    tokens = mems * small
    dma = pltpu.SemaphoreType.DMA
    back = pl.pallas_call(
        functools.partial(column_kernel, mems, grps, frames, rows, steps),
        out_shape=jax.ShapeDtypeStruct((places, small, width), video.dtype),
        in_specs=[pl.BlockSpec(memory_space=pl.ANY)] * 3,
        out_specs=pl.BlockSpec(memory_space=pl.ANY),
        scratch_shapes=[
            pltpu.VMEM((small, places, width), video.dtype),
            pltpu.VMEM((width // LANES, small * places, LANES), jnp.float32),
            pltpu.VMEM((places, small, width), video.dtype),
            pltpu.VMEM((places, small, width), video.dtype),
            pltpu.VMEM(w_triple.shape, w_triple.dtype),
            pltpu.VMEM(w_out.shape, w_out.dtype),
            pltpu.VMEM((tokens, tokens), jnp.float32),
            pltpu.VMEM((tokens, width), video.dtype),
            pltpu.VMEM((tokens, width), video.dtype),
            dma,
            dma((2, 2)),
            dma((places,)),
            dma((places,)),
            dma((places,)),
            dma((places,)),
            pltpu.SemaphoreType.REGULAR,
        ],
        compiler_params=pltpu.CompilerParams(
            collective_id=0, has_side_effects=True, vmem_limit_bytes=50 * 2**20
        ),
    )(video.reshape(small, cols, width), w_triple, w_out)
    return jnp.transpose(back.reshape(cols, frames, rows, width), (1, 2, 0, 3))


def attend_local(triple, forms):
    lead = triple.shape[:-1]
    width = triple.shape[-1] // 3
    pieces = triple.reshape(lead + (3, HEADS, HEAD))
    query = pieces[..., 0, :, :]
    keys = pieces[..., 1, :, :]
    values = pieces[..., 2, :, :]
    scores = jnp.einsum(forms[0], query, keys, preferred_element_type=jnp.float32) * (
        1.0 / HEAD**0.5
    )
    top = jnp.max(scores, axis=-1, keepdims=True)
    expo = jnp.exp(scores - top)
    probs = (expo / jnp.sum(expo, axis=-1, keepdims=True)).astype(jnp.bfloat16)
    context = jnp.einsum(forms[1], probs, values, preferred_element_type=jnp.float32)
    return context.astype(jnp.bfloat16).reshape(lead + (width,))


def make_triple(state, weight_in):
    width = state.shape[-1]
    floats = state.astype(jnp.float32)
    normed = (floats * lax.rsqrt(jnp.mean(floats * floats, axis=-1, keepdims=True) + eps)).astype(
        jnp.bfloat16
    )
    triple = jnp.dot(normed.reshape(-1, width), weight_in, preferred_element_type=jnp.float32)
    return triple.astype(jnp.bfloat16).reshape(state.shape[:-1] + (3 * width,))


def add_update(state, context, weight_back):
    width = state.shape[-1]
    update = jnp.dot(context.reshape(-1, width), weight_back, preferred_element_type=jnp.float32)
    return (state.astype(jnp.float32) + update.reshape(state.shape)).astype(jnp.bfloat16)


def whole_block(state, weight_in, weight_back, forms):
    context = attend_local(make_triple(state, weight_in), forms)
    return add_update(state, context, weight_back)


def by_lines(video, w_triple, w_out):
    regrouped = whole_block(
        lax.all_to_all(video, "mem", split_axis=2, concat_axis=0, tiled=True),
        w_triple[0],
        w_out[0],
        time_forms,
    )
    height_done = whole_block(
        lax.all_to_all(regrouped, "grp", split_axis=0, concat_axis=1, tiled=True),
        w_triple[1],
        w_out[1],
        height_forms,
    )
    return lax.all_to_all(
        lax.all_to_all(height_done, "grp", split_axis=1, concat_axis=0, tiled=True),
        "mem",
        split_axis=0,
        concat_axis=2,
        tiled=True,
    )


def solution(mesh):
    mems, grps = mesh.shape["mem"], mesh.shape["grp"]

    def on_device(video, w_triple, w_out):
        if video.shape[2] == mems * grps and mems == 4 * (mems // 4) == (mems // 4) * grps and grps % CORES == 0:
            return by_column(mems, grps, video, w_triple, w_out)
        return by_lines(video, w_triple, w_out)

    return jax.shard_map(
        on_device,
        mesh=mesh,
        in_specs=(P("mem", "grp", None, None), P(), P()),
        out_specs=P("mem", "grp", None, None),
        check_vma=False,
    )
```

```python
import functools

import jax
import jax.numpy as jnp
from jax import lax
from jax.experimental import pallas as pl
from jax.experimental.pallas import tpu as pltpu
from jax.sharding import PartitionSpec as P

HEADS = 16
HEAD = 64
CORES = 2
LANES = 128

eps = 1e-06
MASKED = -1e30
time_forms = ("sabhe,tabhe->abhst", "abhst,tabhe->sabhe")
height_forms = ("asbhe,atbhe->abhst", "abhst,atbhe->asbhe")


def attend_group(state, block, w_in, w_back, bias, normed, context):
    tokens, width = state.shape
    band = min(256, width)
    per_band = band // HEAD
    floats = state.astype(jnp.float32)
    power = jnp.mean(floats * floats, axis=-1, keepdims=True)
    normed[...] = (floats * lax.rsqrt(power + eps)).astype(jnp.bfloat16)
    lane_head = lax.broadcasted_iota(jnp.int32, (tokens, band), 1) // HEAD
    for start in range(0, width, band):
        pieces = [
            jnp.dot(
                normed[...],
                w_in[block, :, which * width + start : which * width + start + band],
                preferred_element_type=jnp.float32,
            ).astype(jnp.bfloat16)
            for which in range(3)
        ]
        query, keys, values = pieces
        alone = jnp.concatenate(
            [jnp.where(lane_head == head, query, jnp.zeros_like(query)) for head in range(per_band)], axis=0
        )
        scores = lax.dot_general(
            alone, keys, (((1,), (1,)), ((), ())), preferred_element_type=jnp.float32
        )
        expos, shares = [], []
        for head in range(per_band):
            block_scores = scores[head * tokens : (head + 1) * tokens] + bias[...]
            top = jnp.max(block_scores, axis=-1, keepdims=True)
            expo = jnp.exp((block_scores - top) * (1.0 / HEAD**0.5))
            shares.append(1.0 / jnp.sum(expo, axis=-1, keepdims=True))
            expos.append(expo.astype(jnp.bfloat16))
        parts = jnp.dot(jnp.concatenate(expos, axis=0), values, preferred_element_type=jnp.float32)
        mixed = parts[:tokens] * shares[0]
        for head in range(1, per_band):
            part = parts[head * tokens : (head + 1) * tokens] * shares[head]
            mixed = jnp.where(lane_head == head, part, mixed)
        context[:, start : start + band] = mixed.astype(jnp.bfloat16)
    update = jnp.dot(context[...], w_back[block], preferred_element_type=jnp.float32)
    return (state.astype(jnp.float32) + update).astype(jnp.bfloat16)


def line_bias(bias, line_of):
    shape = bias.shape
    first = line_of(lax.broadcasted_iota(jnp.int32, shape, 0))
    second = line_of(lax.broadcasted_iota(jnp.int32, shape, 1))
    bias[...] = jnp.where(first == second, 0.0, MASKED).astype(jnp.float32)


def split_lanes(rows):
    return jnp.stack([rows[:, at : at + LANES] for at in range(0, rows.shape[1], LANES)])


LEVELS = 4
SAME, HALF, LOWER, UPPER = 0, 1, 2, 3
INNER_ORDER = (
    (LOWER, 0, 0), (UPPER, 0, 0), (LOWER, 0, 1), (UPPER, 0, 1), (HALF, 0, 0), (SAME, 0, 0), (HALF, 0, 1), (SAME, 0, 1),
    (LOWER, 1, 0), (UPPER, 1, 0), (LOWER, 1, 1), (UPPER, 1, 1), (HALF, 1, 0), (SAME, 1, 0), (HALF, 1, 1), (SAME, 1, 1),
)
OUTER_ORDER = (
    (HALF, 0, 0), (HALF, 0, 1), (HALF, 1, 0), (HALF, 1, 1), (LOWER, 0, 0), (UPPER, 0, 0), (SAME, 0, 0), (LOWER, 0, 1),
    (UPPER, 0, 1), (SAME, 0, 1), (SAME, 1, 0), (SAME, 1, 1), (LOWER, 1, 0), (UPPER, 1, 0), (LOWER, 1, 1), (UPPER, 1, 1),
)
HELD = 4
HELD_TURNS = 1


def looked_up(at, table):
    found = table[0]
    for index in range(1, len(table)):
        found = jnp.where(at == index, table[index], found)
    return found


def level_of(kind, level):
    near = level + kind - 2 * kind * (level % 2)
    far = (1 - level // 2) * 2 + kind - LOWER
    return jnp.where(kind < LOWER, near, far)


def column_kernel(
    mems, grps, frames, rows, steps,
    x_ref, w_in_hbm, w_back_hbm, out_ref,
    tokens_in, wide, apart, held, w_in, w_back, bias, normed, context,
    x_sem, w_sem, send_in, recv_in, send_out, recv_out, go,
):
    places = mems * grps
    small, width = held.shape[1], held.shape[2]
    per_step = mems // steps
    my_mem, my_grp = lax.axis_index("mem"), lax.axis_index("grp")
    me = my_mem * grps + my_grp
    my_pair, my_part = my_grp // CORES, my_mem // per_step
    outer = (my_part + my_part // 2) % 2 == 0

    arrive = pltpu.make_async_copy(x_ref, tokens_in, x_sem)
    arrive.start()
    weights = []
    for block in range(2):
        weights.append(pltpu.make_async_copy(w_in_hbm.at[block], w_in.at[block], w_sem.at[block, 0]))
        weights.append(pltpu.make_async_copy(w_back_hbm.at[block], w_back.at[block], w_sem.at[block, 1]))
    barrier = pltpu.get_barrier_semaphore()

    @pl.loop(1, places)
    def _(offset):
        other = (me + offset) % places
        pl.semaphore_signal(barrier, inc=1, device_id={"mem": other // grps, "grp": other % grps})

    arrive.wait()
    for copy in weights:
        copy.start()

    @pl.loop(0, small)
    def _(at):
        wide[:, pl.ds(pl.multiple_of(at * places, places), places), :] = split_lanes(
            tokens_in[at].astype(jnp.float32)
        )

    pl.semaphore_wait(barrier, places - 1)

    def inward(place):
        return pltpu.make_async_remote_copy(
            src_ref=apart.at[place],
            dst_ref=held.at[me],
            send_sem=send_in.at[place],
            recv_sem=recv_in.at[me],
            device_id={"mem": place // grps, "grp": place % grps},
        )

    def place_of(at):
        turn = at // per_step
        kind, core, pair = (
            jnp.where(outer, looked_up(turn, [a[k] for a in OUTER_ORDER]), looked_up(turn, [a[k] for a in INNER_ORDER]))
            for k in range(3)
        )
        to_pair = (my_pair + pair) % (grps // CORES)
        to_mem = level_of(kind, my_part) * per_step + (my_mem + at) % per_step
        return to_mem * grps + to_pair * CORES + core

    held_back = places - places // HELD
    my_core = my_grp % CORES

    def start_held():
        @pl.loop(held_back, places)
        def _(at):
            inward(place_of(at)).start()

    @pl.loop(0, places)
    def _(at):
        place = place_of(at)
        for lane in range(wide.shape[0]):
            column = wide[lane, pl.ds(place, small, stride=places), :]
            apart[place, :, lane * LANES : (lane + 1) * LANES] = column.astype(apart.dtype)

        @pl.when(place == me)
        def _():
            pltpu.make_async_copy(apart.at[me], held.at[me], recv_in.at[me]).start()

        @pl.when((place != me) & ~(outer & (at >= held_back)))
        def _():
            inward(place).start()

    @pl.when(outer & (my_core == 1))
    def _():
        pl.semaphore_wait(go, 1)
        start_held()

    line_bias(bias, lambda at: at % rows)
    weights[0].wait()
    weights[1].wait()

    @pl.loop(0, grps)
    def _(turn):
        pair = (my_pair + turn // CORES) % (grps // CORES)
        grp = pair * CORES + (my_grp + turn) % CORES

        @pl.loop(0, mems)
        def _(mem):
            place = mem * grps + grp
            pltpu.make_async_copy(apart.at[place], held.at[place], recv_in.at[place]).wait()

        state = jnp.concatenate([held[mem * grps + grp] for mem in range(mems)], axis=0)
        done = attend_group(state, 0, w_in, w_back, bias, normed, context)
        for mem in range(mems):
            held[mem * grps + grp] = done[mem * small : (mem + 1) * small]

        @pl.when(outer & (my_core == 0) & (turn == HELD_TURNS - 1))
        def _():
            pl.semaphore_signal(go, inc=1, device_id={"mem": my_mem, "grp": my_grp + 1})
            start_held()

    line_bias(bias, lambda at: at // (grps * small) * frames + at // rows % frames)
    weights[2].wait()
    weights[3].wait()

    def outward(place):
        return pltpu.make_async_remote_copy(
            src_ref=held.at[place],
            dst_ref=out_ref.at[me],
            send_sem=send_out.at[place],
            recv_sem=recv_out.at[me],
            device_id={"mem": place // grps, "grp": place % grps},
        )

    count = per_step * grps

    @pl.loop(0, steps)
    def _(turn):
        late = outer & (my_core == 0)
        kind = jnp.where(
            late, looked_up(turn, [HALF, LOWER, UPPER, SAME]), looked_up(turn, [LOWER, UPPER, HALF, SAME])
        )
        step = level_of(kind, my_part)
        first = step * count
        state = jnp.concatenate([held[first + at] for at in range(count)], axis=0)
        done = attend_group(state, 1, w_in, w_back, bias, normed, context)
        for at in range(count):
            held[first + at] = done[at * small : (at + 1) * small]

        @pl.loop(0, count)
        def _(at):
            to_mem = (my_mem + at) % per_step
            to_pair = (my_pair + at // per_step) % (grps // CORES)
            place = first + to_mem * grps + to_pair * CORES + (my_core + at // grps) % CORES

            @pl.when(place == me)
            def _():
                pltpu.make_async_copy(held.at[me], out_ref.at[me], recv_out.at[me]).start()

            @pl.when(place != me)
            def _():
                outward(place).start()

    @pl.loop(1, places)
    def _(offset):
        place = (me + offset) % places
        inward(place).wait_send()
        outward(place).wait_send()

    @pl.loop(0, places)
    def _(place):
        pltpu.make_async_copy(held.at[place], out_ref.at[place], recv_out.at[place]).wait()


def by_column(mems, grps, video, w_triple, w_out):
    frames, rows, cols, width = video.shape
    places, small = mems * grps, frames * rows
    steps = LEVELS
    tokens = mems * small
    dma = pltpu.SemaphoreType.DMA
    back = pl.pallas_call(
        functools.partial(column_kernel, mems, grps, frames, rows, steps),
        out_shape=jax.ShapeDtypeStruct((places, small, width), video.dtype),
        in_specs=[pl.BlockSpec(memory_space=pl.ANY)] * 3,
        out_specs=pl.BlockSpec(memory_space=pl.ANY),
        scratch_shapes=[
            pltpu.VMEM((small, places, width), video.dtype),
            pltpu.VMEM((width // LANES, small * places, LANES), jnp.float32),
            pltpu.VMEM((places, small, width), video.dtype),
            pltpu.VMEM((places, small, width), video.dtype),
            pltpu.VMEM(w_triple.shape, w_triple.dtype),
            pltpu.VMEM(w_out.shape, w_out.dtype),
            pltpu.VMEM((tokens, tokens), jnp.float32),
            pltpu.VMEM((tokens, width), video.dtype),
            pltpu.VMEM((tokens, width), video.dtype),
            dma,
            dma((2, 2)),
            dma((places,)),
            dma((places,)),
            dma((places,)),
            dma((places,)),
            pltpu.SemaphoreType.REGULAR,
        ],
        compiler_params=pltpu.CompilerParams(
            collective_id=0, has_side_effects=True, vmem_limit_bytes=50 * 2**20
        ),
    )(video.reshape(small, cols, width), w_triple, w_out)
    return jnp.transpose(back.reshape(cols, frames, rows, width), (1, 2, 0, 3))


def attend_local(triple, forms):
    lead = triple.shape[:-1]
    width = triple.shape[-1] // 3
    pieces = triple.reshape(lead + (3, HEADS, HEAD))
    query = pieces[..., 0, :, :]
    keys = pieces[..., 1, :, :]
    values = pieces[..., 2, :, :]
    scores = jnp.einsum(forms[0], query, keys, preferred_element_type=jnp.float32) * (
        1.0 / HEAD**0.5
    )
    top = jnp.max(scores, axis=-1, keepdims=True)
    expo = jnp.exp(scores - top)
    probs = (expo / jnp.sum(expo, axis=-1, keepdims=True)).astype(jnp.bfloat16)
    context = jnp.einsum(forms[1], probs, values, preferred_element_type=jnp.float32)
    return context.astype(jnp.bfloat16).reshape(lead + (width,))


def make_triple(state, weight_in):
    width = state.shape[-1]
    floats = state.astype(jnp.float32)
    normed = (floats * lax.rsqrt(jnp.mean(floats * floats, axis=-1, keepdims=True) + eps)).astype(
        jnp.bfloat16
    )
    triple = jnp.dot(normed.reshape(-1, width), weight_in, preferred_element_type=jnp.float32)
    return triple.astype(jnp.bfloat16).reshape(state.shape[:-1] + (3 * width,))


def add_update(state, context, weight_back):
    width = state.shape[-1]
    update = jnp.dot(context.reshape(-1, width), weight_back, preferred_element_type=jnp.float32)
    return (state.astype(jnp.float32) + update.reshape(state.shape)).astype(jnp.bfloat16)


def whole_block(state, weight_in, weight_back, forms):
    context = attend_local(make_triple(state, weight_in), forms)
    return add_update(state, context, weight_back)


def by_lines(video, w_triple, w_out):
    regrouped = whole_block(
        lax.all_to_all(video, "mem", split_axis=2, concat_axis=0, tiled=True),
        w_triple[0],
        w_out[0],
        time_forms,
    )
    height_done = whole_block(
        lax.all_to_all(regrouped, "grp", split_axis=0, concat_axis=1, tiled=True),
        w_triple[1],
        w_out[1],
        height_forms,
    )
    return lax.all_to_all(
        lax.all_to_all(height_done, "grp", split_axis=1, concat_axis=0, tiled=True),
        "mem",
        split_axis=0,
        concat_axis=2,
        tiled=True,
    )


def solution(mesh):
    mems, grps = mesh.shape["mem"], mesh.shape["grp"]

    def on_device(video, w_triple, w_out):
        if video.shape[2] == mems * grps and mems == 4 * (mems // 4) == (mems // 4) * grps and grps % CORES == 0:
            return by_column(mems, grps, video, w_triple, w_out)
        return by_lines(video, w_triple, w_out)

    return jax.shard_map(
        on_device,
        mesh=mesh,
        in_specs=(P("mem", "grp", None, None), P(), P()),
        out_specs=P("mem", "grp", None, None),
        check_vma=False,
    )
```
